128 devices in a mesh: sec: 4 (over y), dev: 32 (over z, x, core).
Axes of the slice: x: 4, y: 4, z: 4, core: 2. Of those that a mesh axis runs over, the one named last changes fastest.
Arguments:
- hidden: bfloat16 [2048, 3584], P(('sec', 'dev')), may hold values from -6 to 6
- expert_ids: int32 [2048, 8], P(('sec', 'dev')), may hold values from 0 to 127, all different within a row; in each aligned block of 16 rows (0 to 15, 16 to 31, ...) at most 2 rows name the same one
- route_weights: float32 [2048, 8], P(('sec', 'dev')), may hold values from 0.1 to 1
- w_gate_up: bfloat16 [128, 3584, 2048], P(('sec', 'dev')), may hold values from -0.09375 to 0.09375
- w_down: bfloat16 [128, 1024, 3584], P(('sec', 'dev')), may hold values from -0.1875 to 0.1875
- query_latent: bfloat16 [512, 128, 512], P(('sec', 'dev')), may hold values from -400 to 400
- query_rope: bfloat16 [512, 64, 128], P(('sec', 'dev')), may hold values from -6 to 6
- latent_cache: bfloat16 [512, 512, 512], P(('sec', 'dev')), may hold values from -4 to 4
- rope_cache: bfloat16 [512, 64, 512], P(('sec', 'dev')), may hold values from -6 to 6
- cache_lengths: int32 [512], P(('sec', 'dev')), may hold values from 64 to 512
Outputs:
- moe_out: bfloat16 [2048, 3584], P(('sec', 'dev'))
- expert_load: float32 [128], replicated
- attention_out: bfloat16 [512, 128, 512], P(('sec', 'dev'))
The draws below stay inside these ranges and needn't reach their ends.
Inputs may be any that keep to these rules, and one draw needn't show every extreme that they name: `expert_ids`: in the rows of one device no expert is named more than 2 times; in some device's rows some expert is named exactly 2 times.
All inputs are finite; a program needn't handle non-finite values.
Results may differ from the reference program's by a relative error of at most 0.008.
Values may be sent and summed in bfloat16 or wider, within the bound.
No kernel may reach another device: no remote copies, remote signals or barrier semaphores. Data moves between devices by JAX's collectives and lax.ppermute only.
A program may use at most 128 MiB of HBM per device.

```python
import math
import jax
import jax.numpy as jnp
import numpy as np
from jax import lax

D = 3584
FF = 1024
TOPK = 8
HEADS = 128
LATENT = 512
ROPE = 64
LEN = 512
ROWS_DEV = 16
EXPERTS = 128
CAP = 2
TOKENS = 2048
ATT_TOTAL = 512


def attention_pair(key):
    cache_key = jax.random.fold_in(key, 11)
    query_key = jax.random.fold_in(key, 12)
    latent = jnp.clip(jax.random.normal(cache_key, (ATT_TOTAL, LEN, LATENT), jnp.float32), -4.0, 4.0)
    queries = jnp.clip(jax.random.normal(query_key, (ATT_TOTAL, HEADS, LATENT), jnp.float32), -4.0, 4.0)
    return (latent, queries)


def draw_latent_cache(key, part):
    return attention_pair(key)[0].astype(jnp.bfloat16)


def draw_query_latent(key, part):
    return attention_pair(key)[1].astype(jnp.bfloat16)


def draw_cache_lengths(key, part):
    length_key = jax.random.fold_in(key, 21)
    lengths = jax.random.randint(length_key, (ATT_TOTAL,), max(6, LEN // 8), LEN + 1, dtype=jnp.int32)
    return lengths.at[0].set(LEN)


def steps_of(own_key, shape, pieces, least, high):
    factor_of, own = 1.0, jax.random.fold_in(own_key, 6)
    for dim, parts in pieces:
        draws = jnp.exp(jax.random.uniform(jax.random.fold_in(own, dim), (parts,), jnp.float32, least / len(pieces), high / len(pieces)))
        factor_of = factor_of * jnp.repeat(draws, shape[dim] // parts).reshape([-1 if axis == dim else 1 for axis in range(len(shape))])
    return factor_of


def shared_out(stream_key, own, number, rows, count, top, bound, lean):
    ranking = jax.random.permutation(stream_key, count)
    packed, ordinary = shares(count, rows * top, bound, lean, True), shares(count, rows * top, bound, lean, False)
    places = jnp.arange(count)

    def named(sizes, rotation):
        used = int((sizes > 0).sum())
        fixed = max(1, used // 4)
        moved = fixed + (places - fixed + rotation * (used - fixed)) % max(1, count - fixed)
        return jnp.zeros((count,), jnp.int32).at[ranking[jnp.where(places < fixed, places, moved)]].set(jnp.asarray(sizes, jnp.int32))

    sizes = jnp.where(number % 4 == 0, named(packed, number // 4), named(ordinary, number - number // 4 - 1))
    mixed = jax.random.permutation(jax.random.fold_in(own, 3), count)
    giver, taker = mixed[0:count // 2 * 2:2], mixed[1:count // 2 * 2:2]
    slack = jnp.minimum(sizes[giver] - 1, bound - sizes[taker]) // 2
    slack = jnp.where((giver == ranking[0]) | (taker == ranking[0]) | (sizes[taker] == 0), 0, jnp.maximum(slack, 0))
    moved = jax.random.randint(jax.random.fold_in(own, 4), (count // 2,), 0, 1 << 20) % (slack + 1)
    sizes = sizes.at[giver].add(-moved).at[taker].add(moved)
    items = jnp.searchsorted(jnp.cumsum(sizes), jnp.arange(rows * top), side="right").astype(jnp.int32)
    grid = items.reshape(top, rows).T
    grid = grid[jax.random.permutation(jax.random.fold_in(own, 1), rows)]
    rotation = jax.random.randint(jax.random.fold_in(own, 2), (rows, 1), 0, top)
    return jnp.take_along_axis(grid, (jnp.arange(top)[None, :] + rotation) % top, axis=1)


def shares(number_of, total, limit, lean, full):
    loads = [(1 << 20) // math.isqrt(grade ** lean) + 1 for grade in range(1, number_of + 1)]
    largest = limit if full else min(limit, max(-(-total // number_of), total * loads[0] // sum(loads)))
    least = 1 if total - largest >= number_of - 1 else 0
    holding, rest = [largest] + [least] * (number_of - 1), total - largest - least * (number_of - 1)
    while rest > 0:
        movable = [i for i in range(1, number_of) if holding[i] < largest] or [i for i in range(1, number_of) if holding[i] < limit]
        pool, remaining = sum([loads[i] for i in movable]), rest
        for i in movable:
            extra = min(limit - holding[i], max(1, remaining * loads[i] // pool), rest)
            holding[i] = holding[i] + extra
            rest = rest - extra
    return np.array(holding)


def gaussian(own_key, shape, scale, limit, shards=(), kind=jnp.bfloat16):
    values = jax.random.normal(own_key, shape, jnp.float32) * scale
    if len(shards) > 0:
        values = steps_of(own_key, shape, shards, -0.22, 0.18) * values
    return jnp.clip(values, min=-limit, max=limit).astype(kind)


def setup_inputs(seed: int = 0) -> dict:
    seeds = jax.random.split(jax.random.key(seed), 11)
    hidden = gaussian(seeds[0], (TOKENS, D), 1.0, 6.0, ((0, 128),))
    expert_ids_keys = jax.random.split(jax.random.fold_in(seeds[1], 1), TOKENS // ROWS_DEV)
    expert_ids_turns = jax.random.permutation(jax.random.fold_in(seeds[1], 3), TOKENS // ROWS_DEV)
    expert_ids = jax.vmap(lambda own, number: shared_out(jax.random.fold_in(seeds[1], 2), own, number, ROWS_DEV, EXPERTS, TOPK, CAP, 2))(expert_ids_keys, expert_ids_turns).reshape((TOKENS, TOPK))
    route_weights = jnp.clip(0.1 + 0.9 * jax.random.uniform(seeds[2], (TOKENS, TOPK), jnp.float32) ** steps_of(seeds[2], (TOKENS, TOPK), ((0, 128),), -0.2, 0.2), 0.1, 1.0)
    w_gate_up = gaussian(seeds[3], (EXPERTS, D, 2 * FF), D ** -0.5, 0.09375, ((0, 128),))
    w_down = gaussian(seeds[4], (EXPERTS, FF, D), FF ** -0.5, 0.1875, ((0, 128),))
    query_latent = draw_query_latent(jax.random.fold_in(seeds[10], 71), 0)
    query_rope = gaussian(seeds[6], (ATT_TOTAL, ROPE, HEADS), 1.0, 6.0, ((0, 128),))
    latent_cache = draw_latent_cache(jax.random.fold_in(seeds[10], 71), 0)
    rope_cache = gaussian(seeds[8], (ATT_TOTAL, ROPE, LEN), 1.0, 6.0, ((0, 128),))
    cache_lengths = draw_cache_lengths(jax.random.fold_in(seeds[10], 71), 0)
    return {"hidden": hidden, "expert_ids": expert_ids, "route_weights": route_weights, "w_gate_up": w_gate_up, "w_down": w_down, "query_latent": query_latent, "query_rope": query_rope, "latent_cache": latent_cache, "rope_cache": rope_cache, "cache_lengths": cache_lengths}


def attend(query_latent, query_rope, latent_cache, rope_cache, cache_lengths):
    factor = (query_latent.shape[2] + query_rope.shape[1]) ** -0.5
    scores = jnp.einsum("rhc,rtc->rht", query_latent.astype(jnp.float32), latent_cache.astype(jnp.float32))
    scores = scores + jnp.einsum("rph,rpt->rht", query_rope.astype(jnp.float32), rope_cache.astype(jnp.float32))
    scores = scores * factor
    positions = jnp.arange(latent_cache.shape[1], dtype=jnp.int32)
    live_mask = positions[None, None, :] < cache_lengths.astype(jnp.int32)[:, None, None]
    scores = jnp.where(live_mask, scores, -1e30)
    highest = jnp.max(scores, axis=-1, keepdims=True)
    powers = jnp.exp(scores - highest)
    attention_weights = (powers / jnp.sum(powers, axis=-1, keepdims=True)).astype(jnp.bfloat16)
    result = jnp.einsum("rht,rtc->rhc", attention_weights.astype(jnp.float32), latent_cache.astype(jnp.float32))
    return result.astype(jnp.bfloat16)


def reference(hidden, expert_ids, route_weights, w_gate_up, w_down, query_latent, query_rope, latent_cache, rope_cache, cache_lengths):
    token_count, model_width = hidden.shape
    experts = w_gate_up.shape[0]
    hidden_units = w_down.shape[1]
    blocks = token_count // ROWS_DEV
    grouped = expert_ids.reshape(blocks, ROWS_DEV * TOPK).astype(jnp.int32)
    onehot = (grouped[:, :, None] == jnp.arange(experts, dtype=jnp.int32)[None, None, :]).astype(jnp.int32)
    earlier = jnp.cumsum(onehot, axis=1) - onehot
    rank_in = jnp.sum(earlier * onehot, axis=2)
    position = (jnp.arange(blocks, dtype=jnp.int32)[:, None] * CAP + rank_in).reshape(-1).astype(jnp.int32)
    flat_ids = expert_ids.reshape(-1).astype(jnp.int32)
    row_index = (jnp.arange(token_count * TOPK, dtype=jnp.int32) // TOPK).astype(jnp.int32)
    slot_table = jnp.zeros((experts, blocks * CAP), jnp.int32).at[flat_ids, position].set(row_index)
    weight_table = jnp.zeros((experts, blocks * CAP), jnp.float32).at[flat_ids, position].set(route_weights.reshape(-1))

    def one_expert(accumulated, expert):
        chosen_rows = slot_table[expert]
        inputs = hidden[chosen_rows]
        projected = jnp.dot(inputs, w_gate_up[expert], preferred_element_type=jnp.float32)
        activated = (jax.nn.silu(projected[:, :hidden_units]) * projected[:, hidden_units:]).astype(jnp.bfloat16)
        produced = jnp.dot(activated, w_down[expert], preferred_element_type=jnp.float32).astype(jnp.bfloat16)
        accumulated = accumulated.at[chosen_rows].add(weight_table[expert][:, None] * produced.astype(jnp.float32))
        return accumulated, None

    accumulated, unused = lax.scan(one_expert, jnp.zeros((token_count, model_width), jnp.float32), jnp.arange(experts, dtype=jnp.int32))
    moe_out = accumulated.astype(jnp.bfloat16)
    counts = jnp.sum(onehot, axis=(0, 1)).astype(jnp.float32)
    expert_load = counts / (token_count * TOPK / experts)
    attention_out = attend(query_latent, query_rope, latent_cache, rope_cache, cache_lengths)
    return (moe_out, expert_load, attention_out)
```

```python
import functools

import jax
import jax.numpy as jnp
from jax import lax
from jax.experimental import pallas as pl
from jax.experimental.pallas import tpu as pltpu
from jax.sharding import PartitionSpec as P

LANES = 128
BF16 = jnp.bfloat16
F32 = jnp.float32


def iota(shape, axis):
    return lax.broadcasted_iota(jnp.int32, shape, axis)


def packed_place(tile_row, blocks):
    within = tile_row & 7
    return (within >> 1) * (2 * blocks) + (tile_row >> 3) * 2 + (within & 1)


def to_rows_matrix(blocks):
    size = 8 * blocks
    return jnp.where(packed_place(iota((size, size), 0), blocks) == iota((size, size), 1), 1.0, 0.0).astype(BF16)


def to_chunks_matrix(blocks):
    size = 8 * blocks
    return jnp.where(packed_place(iota((size, size), 1), blocks) == iota((size, size), 0), 1.0, 0.0).astype(BF16)


def chunks_to_rows(chunk_ref, rows_ref, blocks):
    size = 8 * blocks
    matrix = to_rows_matrix(blocks)

    def step(group, carry):
        start = pl.multiple_of(group * (2 * size), 16)
        packed = chunk_ref[pl.ds(start, 2 * size), :].astype(F32)
        pair = jnp.concatenate([packed[:size], packed[size:]], axis=1).astype(BF16)
        spread = jnp.dot(matrix, pair, preferred_element_type=F32)
        row = pl.multiple_of(group * 16, 16)
        for block in range(blocks):
            piece = spread[8 * block : 8 * block + 8]
            rows_ref[pl.ds(row, 16), LANES * block : LANES * (block + 1)] = jnp.concatenate(
                [piece[:, :LANES], piece[:, LANES:]], axis=0
            ).astype(rows_ref.dtype)
        return carry

    lax.fori_loop(0, chunk_ref.shape[0] // (2 * size), step, 0)


def rows_to_chunks(rows_ref, chunk_ref, blocks):
    size = 8 * blocks
    matrix = to_chunks_matrix(blocks)

    def step(group, carry):
        row = pl.multiple_of(group * 16, 16)
        first = jnp.concatenate(
            [rows_ref[pl.ds(row, 8), LANES * b : LANES * (b + 1)] for b in range(blocks)], axis=0
        )
        second = jnp.concatenate(
            [rows_ref[pl.ds(row + 8, 8), LANES * b : LANES * (b + 1)] for b in range(blocks)], axis=0
        )
        pair = jnp.concatenate([first, second], axis=1).astype(BF16)
        packed = jnp.dot(matrix, pair, preferred_element_type=F32)
        start = pl.multiple_of(group * (2 * size), 16)
        chunk_ref[pl.ds(start, 2 * size), :] = jnp.concatenate(
            [packed[:, :LANES], packed[:, LANES:]], axis=0
        ).astype(BF16)
        return carry

    lax.fori_loop(0, chunk_ref.shape[0] // (2 * size), step, 0)


def choices(ids, values):
    lane = iota((ids.shape[0], LANES), 1)
    total = jnp.zeros((ids.shape[0], LANES), F32)
    for k in range(ids.shape[1]):
        total = total + jnp.where(ids[:, k : k + 1] == lane, values[k], 0.0)
    return total


def slot_of(chosen):
    rows = chosen.shape[0]
    before = jnp.where(iota((rows, rows), 1) < iota((rows, rows), 0), 1.0, 0.0).astype(BF16)
    return jnp.dot(before, chosen.astype(BF16), preferred_element_type=F32)


def interleave(first, second):
    experts = first.shape[1]
    expert, place = iota((experts, 2 * experts), 0), iota((experts, 2 * experts), 1)
    even = jnp.where(place == 2 * expert, 1.0, 0.0).astype(BF16)
    odd = jnp.where(place == 2 * expert + 1, 1.0, 0.0).astype(BF16)
    return jnp.dot(first.astype(BF16), even, preferred_element_type=F32) + jnp.dot(
        second.astype(BF16), odd, preferred_element_type=F32
    )


def dispatch_kernel(ids_ref, hidden_ref, chunk_ref, rows_ref):
    ids = ids_ref[...]
    width = hidden_ref.shape[1]
    chosen = choices(ids, [1.0] * ids.shape[1])
    slot = slot_of(chosen)
    placer = interleave(jnp.where(slot == 0.0, chosen, 0.0), jnp.where(slot == 1.0, chosen, 0.0))
    placer = jnp.transpose(placer).astype(BF16)
    rows_ref[:, :width] = jnp.dot(placer, hidden_ref[...], preferred_element_type=F32)
    counts = jnp.sum(chosen, axis=0, keepdims=True)
    rows_ref[:, width:] = jnp.broadcast_to(counts, (rows_ref.shape[0], LANES))
    rows_to_chunks(rows_ref, chunk_ref, rows_ref.shape[1] // LANES)


def expert_kernel(
    chunk_ref, up_hbm, down_hbm, out_ref, load_ref, up_ref, down_ref, rows_ref, act_ref, made_ref, up_sem, down_sem
):
    ups, downs = up_ref.shape[0], down_ref.shape[0]
    up_width, down_width = up_ref.shape[2], down_ref.shape[2]
    half = ups // 2
    width = up_ref.shape[1]

    def up_copy(c):
        return pltpu.make_async_copy(up_hbm.at[0, :, pl.ds(c * up_width, up_width)], up_ref.at[c], up_sem.at[c])

    def down_copy(c):
        return pltpu.make_async_copy(
            down_hbm.at[0, :, pl.ds(c * down_width, down_width)], down_ref.at[c], down_sem.at[c]
        )

    for c in range(half):
        up_copy(c).start()
        up_copy(c + half).start()
    for c in range(downs):
        down_copy(c).start()

    chunks_to_rows(chunk_ref, rows_ref, rows_ref.shape[1] // LANES)
    counts = jnp.sum(rows_ref[:, width:].astype(F32), axis=0, keepdims=True)
    load_ref[...] = counts * (0.5 / load_ref.shape[1])

    def up_step(c, carry):
        up_copy(c).wait()
        up_copy(c + half).wait()
        rows = rows_ref[:, :width]
        gate = jnp.dot(rows, up_ref[c], preferred_element_type=F32)
        up = jnp.dot(rows, up_ref[c + half], preferred_element_type=F32)
        place = pl.multiple_of(c * up_width, up_width)
        act_ref[:, pl.ds(place, up_width)] = (gate / (1.0 + jnp.exp(-gate)) * up).astype(BF16)
        return carry

    lax.fori_loop(0, half, up_step, 0)

    def down_step(c, carry):
        down_copy(c).wait()
        made = jnp.dot(act_ref[...], down_ref[c], preferred_element_type=F32)
        place = pl.multiple_of(c * down_width, down_width)
        made_ref[:, pl.ds(place, down_width)] = made
        return carry

    lax.fori_loop(0, downs, down_step, 0)
    rows_to_chunks(made_ref, out_ref, made_ref.shape[1] // LANES)


def combine_kernel(ids_ref, weights_ref, chunk_ref, out_ref, rows_ref):
    ids, weights = ids_ref[...], weights_ref[...]
    count = ids.shape[1]
    slot = slot_of(choices(ids, [1.0] * count))
    weight = choices(ids, [weights[:, k : k + 1] for k in range(count)])

    def parts(value):
        high = value.astype(BF16).astype(F32)
        return jnp.concatenate([high, value - high], axis=0)

    mixer = interleave(parts(jnp.where(slot == 0.0, weight, 0.0)), parts(jnp.where(slot == 1.0, weight, 0.0)))
    chunks_to_rows(chunk_ref, rows_ref, rows_ref.shape[1] // LANES)
    mixed = jnp.dot(mixer.astype(BF16), rows_ref[...], preferred_element_type=F32)
    rows = ids.shape[0]
    out_ref[...] = (mixed[:rows] + mixed[rows:]).astype(BF16)


def attend(query_latent, query_rope, latent_cache, rope_cache, cache_lengths):
    factor = (query_latent.shape[2] + query_rope.shape[1]) ** (-0.5)
    scores = jnp.einsum("rhc,rtc->rht", query_latent, latent_cache, preferred_element_type=F32)
    scores = scores + jnp.einsum("rph,rpt->rht", query_rope, rope_cache, preferred_element_type=F32)
    scores = scores * factor
    positions = jnp.arange(latent_cache.shape[1], dtype=jnp.int32)
    live_mask = positions[None, None, :] < cache_lengths[:, None, None]
    scores = jnp.where(live_mask, scores, -1e30)
    highest = jnp.max(scores, axis=-1, keepdims=True)
    powers = jnp.exp(scores - highest)
    attention_weights = (powers / jnp.sum(powers, axis=-1, keepdims=True)).astype(BF16)
    result = jnp.einsum("rht,rtc->rhc", attention_weights, latent_cache, preferred_element_type=F32)
    return result.astype(BF16)


def vmem(count):
    return [pl.BlockSpec(memory_space=pltpu.VMEM)] * count


def exchange(chunks, experts):
    width = chunks.shape[1]
    shaped = chunks.reshape(experts, -1, 2, width)
    moved = lax.all_to_all(shaped, ("sec", "dev"), split_axis=0, concat_axis=0, tiled=True)
    return moved.reshape(chunks.shape)


def per_device(
    hidden,
    expert_ids,
    route_weights,
    w_gate_up,
    w_down,
    query_latent,
    query_rope,
    latent_cache,
    rope_cache,
    cache_lengths,
):
    model_width = hidden.shape[1]
    experts = lax.axis_size("sec") * lax.axis_size("dev")
    slots = 2 * experts
    units = w_down.shape[1]
    blocks = model_width // LANES
    sent = blocks + 1

    outgoing = pl.pallas_call(
        dispatch_kernel,
        out_shape=jax.ShapeDtypeStruct((slots * sent, LANES), BF16),
        in_specs=vmem(2),
        out_specs=pl.BlockSpec(memory_space=pltpu.VMEM),
        scratch_shapes=[pltpu.VMEM((slots, sent * LANES), F32)],
        compiler_params=pltpu.CompilerParams(vmem_limit_bytes=16 << 20),
        name="dispatch",
    )(expert_ids, hidden)
    received = exchange(outgoing, experts)

    up_width, down_width = 256, 512
    ups, downs = 2 * units // up_width, model_width // down_width
    returned, load = pl.pallas_call(
        expert_kernel,
        out_shape=(
            jax.ShapeDtypeStruct((slots * blocks, LANES), BF16),
            jax.ShapeDtypeStruct((1, experts), F32),
        ),
        in_specs=vmem(1) + [pl.BlockSpec(memory_space=pl.ANY)] * 2,
        out_specs=tuple(vmem(2)),
        scratch_shapes=[
            pltpu.VMEM((ups, model_width, up_width), BF16),
            pltpu.VMEM((downs, units, down_width), BF16),
            pltpu.VMEM((slots, sent * LANES), BF16),
            pltpu.VMEM((slots, units), BF16),
            pltpu.VMEM((slots, model_width), F32),
            pltpu.SemaphoreType.DMA((ups,)),
            pltpu.SemaphoreType.DMA((downs,)),
        ],
        compiler_params=pltpu.CompilerParams(vmem_limit_bytes=48 << 20),
        name="experts",
    )(received, w_gate_up, w_down)
    collected = exchange(returned, experts)

    moe_out = pl.pallas_call(
        combine_kernel,
        out_shape=jax.ShapeDtypeStruct(hidden.shape, BF16),
        in_specs=vmem(3),
        out_specs=pl.BlockSpec(memory_space=pltpu.VMEM),
        scratch_shapes=[pltpu.VMEM((slots, model_width), BF16)],
        compiler_params=pltpu.CompilerParams(vmem_limit_bytes=16 << 20),
        name="combine",
    )(expert_ids, route_weights, collected)
    attention_out = attend(query_latent, query_rope, latent_cache, rope_cache, cache_lengths)
    return (moe_out, load[0], attention_out)


def solution(mesh):
    split = ("sec", "dev")
    return jax.shard_map(
        per_device,
        mesh=mesh,
        in_specs=(
            P(split, None),
            P(split, None),
            P(split, None),
            P(split, None, None),
            P(split, None, None),
            P(split, None, None),
            P(split, None, None),
            P(split, None, None),
            P(split, None, None),
            P(split),
        ),
        out_specs=(P(split, None), P(), P(split, None, None)),
        check_vma=False,
    )
```

```python
import jax
import jax.numpy as jnp
from jax import lax
from jax.experimental import pallas as pl
from jax.experimental.pallas import tpu as pltpu
from jax.sharding import Mesh, PartitionSpec as P

LANES = 128
BF16 = jnp.bfloat16
F32 = jnp.float32
IN_FLIGHT = 6
AXES = ("core", "y", "x", "z")


def iota(shape, axis):
    return lax.broadcasted_iota(jnp.int32, shape, axis)


def packed_place(tile_row, blocks):
    within = tile_row & 7
    return (within >> 1) * (2 * blocks) + (tile_row >> 3) * 2 + (within & 1)


def to_rows_matrix(blocks):
    size = 8 * blocks
    return jnp.where(packed_place(iota((size, size), 0), blocks) == iota((size, size), 1), 1.0, 0.0).astype(BF16)


def to_chunks_matrix(blocks):
    size = 8 * blocks
    return jnp.where(packed_place(iota((size, size), 1), blocks) == iota((size, size), 0), 1.0, 0.0).astype(BF16)


def chunks_to_rows(chunk_ref, rows_ref, blocks, before=None):
    size = 8 * blocks
    matrix = to_rows_matrix(blocks)
    for group in range(chunk_ref.shape[0] // (2 * size)):
        if before is not None:
            before(group)
        start, row = group * (2 * size), group * 16
        packed = chunk_ref[start : start + 2 * size, :].astype(F32)
        pair = jnp.concatenate([packed[:size], packed[size:]], axis=1).astype(BF16)
        spread = jnp.dot(matrix, pair, preferred_element_type=F32)
        for block in range(blocks):
            piece = spread[8 * block : 8 * block + 8]
            rows_ref[row : row + 16, LANES * block : LANES * (block + 1)] = jnp.concatenate(
                [piece[:, :LANES], piece[:, LANES:]], axis=0
            ).astype(rows_ref.dtype)


def rows_to_chunks(rows_ref, chunk_ref, blocks, after=None):
    size = 8 * blocks
    matrix = to_chunks_matrix(blocks)
    for group in range(chunk_ref.shape[0] // (2 * size)):
        start, row = group * (2 * size), group * 16
        halves = [
            jnp.concatenate(
                [rows_ref[first : first + 8, LANES * b : LANES * (b + 1)] for b in range(blocks)], axis=0
            )
            for first in (row, row + 8)
        ]
        packed = jnp.dot(matrix, jnp.concatenate(halves, axis=1).astype(BF16), preferred_element_type=F32)
        chunk_ref[start : start + 2 * size, :] = jnp.concatenate(
            [packed[:, :LANES], packed[:, LANES:]], axis=0
        ).astype(BF16)
        if after is not None:
            after(group)


def choices(ids, values):
    lane = iota((ids.shape[0], LANES), 1).astype(ids.dtype)
    total = jnp.zeros((ids.shape[0], LANES), F32)
    for k in range(ids.shape[1]):
        total = total + jnp.where(ids[:, k : k + 1] == lane, values[k], 0.0)
    return total


def rank_of(ids):
    ids = ids.astype(jnp.int32)
    core, x, z, y = ids & 1, (ids >> 1) & 3, (ids >> 3) & 3, ids >> 5
    return ((core * 4 + y) * 4 + x) * 4 + z


def slot_of(chosen):
    rows = chosen.shape[0]
    before = jnp.where(iota((rows, rows), 1) < iota((rows, rows), 0), 1.0, 0.0).astype(BF16)
    return jnp.dot(before, chosen.astype(BF16), preferred_element_type=F32)


def interleave(first, second):
    experts = first.shape[1]
    expert, place = iota((experts, 2 * experts), 0), iota((experts, 2 * experts), 1)
    even = jnp.where(place == 2 * expert, 1.0, 0.0).astype(BF16)
    odd = jnp.where(place == 2 * expert + 1, 1.0, 0.0).astype(BF16)
    return jnp.dot(first.astype(BF16), even, preferred_element_type=F32) + jnp.dot(
        second.astype(BF16), odd, preferred_element_type=F32
    )


def dispatch_kernel(ids_hbm, hidden_hbm, chunk_ref, ids_ref, hidden_ref, rows_ref, sem):
    ids_copy = pltpu.make_async_copy(ids_hbm, ids_ref, sem.at[0])
    hidden_copy = pltpu.make_async_copy(hidden_hbm, hidden_ref, sem.at[1])
    ids_copy.start()
    hidden_copy.start()
    ids_copy.wait()
    count = ids_ref.shape[0]
    ids = jnp.transpose(ids_ref[...].astype(F32))
    width = hidden_ref.shape[1]
    counts = jnp.sum(choices(ids, [1.0] * count), axis=0, keepdims=True)
    chosen = choices(rank_of(ids), [1.0] * count)
    slot = slot_of(chosen)
    placer = interleave(jnp.where(slot == 0.0, chosen, 0.0), jnp.where(slot == 1.0, chosen, 0.0))
    placer = jnp.transpose(placer).astype(BF16)
    rows_ref[:, width:] = jnp.broadcast_to(counts, (rows_ref.shape[0], LANES))
    hidden_copy.wait()
    rows_ref[:, :width] = jnp.dot(placer, hidden_ref[...], preferred_element_type=F32)
    rows_to_chunks(rows_ref, chunk_ref, rows_ref.shape[1] // LANES)


def expert_kernel(
    chunk_ref,
    up_hbm,
    down_hbm,
    out_hbm,
    load_ref,
    up_ref,
    down_ref,
    rows_ref,
    act_ref,
    made_ref,
    out_ref,
    weight_sem,
    out_sem,
):
    ups, downs = up_ref.shape[0], down_ref.shape[0]
    up_width, down_width = up_ref.shape[2], down_ref.shape[2]
    half = ups // 2
    width = up_ref.shape[1]

    copies = []
    for c in range(half):
        for part in (c, c + half):
            copies.append((up_hbm.at[0, :, pl.ds(part * up_width, up_width)], up_ref.at[part]))
    for c in range(downs):
        copies.append((down_hbm.at[0, :, pl.ds(c * down_width, down_width)], down_ref.at[c]))
    copies = [pltpu.make_async_copy(*pair, weight_sem.at[n]) for n, pair in enumerate(copies)]
    for copy in copies[:IN_FLIGHT]:
        copy.start()

    def arrive(n):
        copies[n].wait()
        if n + IN_FLIGHT < len(copies):
            copies[n + IN_FLIGHT].start()

    chunks_to_rows(chunk_ref, rows_ref, rows_ref.shape[1] // LANES)
    counts = jnp.sum(rows_ref[:, width:].astype(F32), axis=0, keepdims=True)
    load_ref[...] = counts * (0.5 / load_ref.shape[1])

    for c in range(half):
        arrive(2 * c)
        arrive(2 * c + 1)
        rows = rows_ref[:, :width]
        gate = jnp.dot(rows, up_ref[c], preferred_element_type=F32)
        up = jnp.dot(rows, up_ref[c + half], preferred_element_type=F32)
        act_ref[:, c * up_width : (c + 1) * up_width] = (gate / (1.0 + jnp.exp(-gate)) * up).astype(BF16)

    for c in range(downs):
        arrive(ups + c)
        made_ref[:, c * down_width : (c + 1) * down_width] = jnp.dot(
            act_ref[...], down_ref[c], preferred_element_type=F32
        )

    blocks = made_ref.shape[1] // LANES
    span = 4 * 16 * blocks
    leave = [
        pltpu.make_async_copy(
            out_ref.at[pl.ds(n * span, span), :], out_hbm.at[pl.ds(n * span, span), :], out_sem.at[n]
        )
        for n in range(out_ref.shape[0] // span)
    ]

    def after(group):
        if group % 4 == 3:
            leave[group // 4].start()

    rows_to_chunks(made_ref, out_ref, blocks, after)
    for copy in leave:
        copy.wait()


def combine_kernel(ids_ref, weights_ref, chunk_hbm, out_ref, chunk_ref, rows_ref, sem):
    blocks = rows_ref.shape[1] // LANES
    span = 4 * 16 * blocks
    enter = [
        pltpu.make_async_copy(
            chunk_hbm.at[pl.ds(n * span, span), :], chunk_ref.at[pl.ds(n * span, span), :], sem.at[n]
        )
        for n in range(chunk_ref.shape[0] // span)
    ]
    for copy in enter:
        copy.start()
    ids, weights = jnp.transpose(ids_ref[...].astype(F32)), jnp.transpose(weights_ref[...])
    count = ids.shape[1]
    ids = rank_of(ids)
    slot = slot_of(choices(ids, [1.0] * count))
    weight = choices(ids, [weights[:, k : k + 1] for k in range(count)])

    def parts(value):
        high = value.astype(BF16).astype(F32)
        return jnp.concatenate([high, value - high], axis=0)

    mixer = interleave(parts(jnp.where(slot == 0.0, weight, 0.0)), parts(jnp.where(slot == 1.0, weight, 0.0)))

    def before(group):
        if group % 4 == 0:
            enter[group // 4].wait()

    chunks_to_rows(chunk_ref, rows_ref, blocks, before)
    mixed = jnp.dot(mixer.astype(BF16), rows_ref[...], preferred_element_type=F32)
    rows = ids.shape[0]
    out_ref[...] = (mixed[:rows] + mixed[rows:]).astype(BF16)


def attend(query_latent, query_rope, latent_cache, rope_cache, cache_lengths):
    factor = (query_latent.shape[2] + query_rope.shape[1]) ** (-0.5)
    scores = jnp.einsum("rhc,rtc->rht", query_latent, latent_cache, preferred_element_type=F32)
    scores = scores + jnp.einsum("rph,rpt->rht", query_rope, rope_cache, preferred_element_type=F32)
    scores = scores * factor
    positions = jnp.arange(latent_cache.shape[1], dtype=jnp.int32)
    live_mask = positions[None, None, :] < cache_lengths[:, None, None]
    scores = jnp.where(live_mask, scores, -1e30)
    highest = jnp.max(scores, axis=-1, keepdims=True)
    powers = jnp.exp(scores - highest)
    attention_weights = (powers / jnp.sum(powers, axis=-1, keepdims=True)).astype(BF16)
    result = jnp.einsum("rht,rtc->rhc", attention_weights, latent_cache, preferred_element_type=F32)
    return result.astype(BF16)


def vmem(count):
    return [pl.BlockSpec(memory_space=pltpu.VMEM)] * count


def hbm(count):
    return [pl.BlockSpec(memory_space=pltpu.HBM)] * count


def exchange(chunks, experts):
    width = chunks.shape[1]
    shaped = chunks.reshape(experts, -1, 2, width)
    moved = lax.all_to_all(shaped, AXES, split_axis=0, concat_axis=0, tiled=True)
    return moved.reshape(chunks.shape)


def per_device(
    hidden,
    expert_ids,
    route_weights,
    w_gate_up,
    w_down,
    query_latent,
    query_rope,
    latent_cache,
    rope_cache,
    cache_lengths,
):
    model_width = hidden.shape[1]
    experts = lax.axis_size(AXES)
    slots = 2 * experts
    units = w_down.shape[1]
    blocks = model_width // LANES
    sent = blocks + 1

    outgoing = pl.pallas_call(
        dispatch_kernel,
        out_shape=jax.ShapeDtypeStruct((slots * sent, LANES), BF16),
        in_specs=hbm(2),
        out_specs=pl.BlockSpec(memory_space=pltpu.VMEM),
        scratch_shapes=[
            pltpu.VMEM(expert_ids.shape[::-1], jnp.int32),
            pltpu.VMEM(hidden.shape, BF16),
            pltpu.VMEM((slots, sent * LANES), F32),
            pltpu.SemaphoreType.DMA((2,)),
        ],
        compiler_params=pltpu.CompilerParams(vmem_limit_bytes=65_110_016),
        name="dispatch",
    )(expert_ids.T, hidden)
    received = exchange(outgoing, experts)

    up_width, down_width = 256, 512
    ups, downs = 2 * units // up_width, model_width // down_width
    returned, load = pl.pallas_call(
        expert_kernel,
        out_shape=(
            jax.ShapeDtypeStruct((slots * blocks, LANES), BF16),
            jax.ShapeDtypeStruct((1, experts), F32),
        ),
        in_specs=vmem(1) + hbm(2),
        out_specs=tuple(hbm(1) + vmem(1)),
        scratch_shapes=[
            pltpu.VMEM((ups, model_width, up_width), BF16),
            pltpu.VMEM((downs, units, down_width), BF16),
            pltpu.VMEM((slots, sent * LANES), BF16),
            pltpu.VMEM((slots, units), BF16),
            pltpu.VMEM((slots, model_width), F32),
            pltpu.VMEM((slots * blocks, LANES), BF16),
            pltpu.SemaphoreType.DMA((ups + downs,)),
            pltpu.SemaphoreType.DMA((4,)),
        ],
        compiler_params=pltpu.CompilerParams(vmem_limit_bytes=60 * 1024 * 1024),
        name="experts",
    )(received, w_gate_up, w_down)
    collected = exchange(returned, experts)

    moe_out = pl.pallas_call(
        combine_kernel,
        out_shape=jax.ShapeDtypeStruct(hidden.shape, BF16),
        in_specs=vmem(2) + hbm(1),
        out_specs=pl.BlockSpec(memory_space=pltpu.VMEM),
        scratch_shapes=[
            pltpu.VMEM((slots * blocks, LANES), BF16),
            pltpu.VMEM((slots, model_width), BF16),
            pltpu.SemaphoreType.DMA((4,)),
        ],
        compiler_params=pltpu.CompilerParams(vmem_limit_bytes=16 << 20),
        name="combine",
    )(expert_ids.T, route_weights.T, collected)
    attention_out = attend(query_latent, query_rope, latent_cache, rope_cache, cache_lengths)
    return (moe_out, load[0], attention_out)


def solution(mesh):
    split = ("y", "z", "x", "core")
    mesh = Mesh(mesh.devices.reshape(4, 4, 4, 2), split)
    return jax.shard_map(
        per_device,
        mesh=mesh,
        in_specs=(
            P(split, None),
            P(split, None),
            P(split, None),
            P(split, None, None),
            P(split, None, None),
            P(split, None, None),
            P(split, None, None),
            P(split, None, None),
            P(split, None, None),
            P(split),
        ),
        out_specs=(P(split, None), P(), P(split, None, None)),
        check_vma=False,
    )
```

```python
import jax
import jax.numpy as jnp
from jax import lax
from jax.experimental import pallas as pl
from jax.experimental.pallas import tpu as pltpu
from jax.sharding import Mesh, PartitionSpec as P

LANES = 128
BF16 = jnp.bfloat16
F32 = jnp.float32
IN_FLIGHT = 6
AXES = ("core", "y", "x", "z")


def iota(shape, axis):
    return lax.broadcasted_iota(jnp.int32, shape, axis)


def packed_place(tile_row, blocks):
    within = tile_row & 7
    return (within >> 1) * (2 * blocks) + (tile_row >> 3) * 2 + (within & 1)


def to_rows_matrix(blocks):
    size = 8 * blocks
    return jnp.where(packed_place(iota((size, size), 0), blocks) == iota((size, size), 1), 1.0, 0.0).astype(BF16)


def to_chunks_matrix(blocks):
    size = 8 * blocks
    return jnp.where(packed_place(iota((size, size), 1), blocks) == iota((size, size), 0), 1.0, 0.0).astype(BF16)


def chunks_to_rows(chunk_ref, rows_ref, blocks, before=None):
    size = 8 * blocks
    matrix = to_rows_matrix(blocks)
    for group in range(chunk_ref.shape[0] // (2 * size)):
        if before is not None:
            before(group)
        start, row = group * (2 * size), group * 16
        packed = chunk_ref[start : start + 2 * size, :].astype(F32)
        pair = jnp.concatenate([packed[:size], packed[size:]], axis=1).astype(BF16)
        spread = jnp.dot(matrix, pair, preferred_element_type=F32)
        for block in range(blocks):
            piece = spread[8 * block : 8 * block + 8]
            rows_ref[row : row + 16, LANES * block : LANES * (block + 1)] = jnp.concatenate(
                [piece[:, :LANES], piece[:, LANES:]], axis=0
            ).astype(rows_ref.dtype)


def rows_to_chunks(rows_ref, chunk_ref, blocks, after=None):
    size = 8 * blocks
    matrix = to_chunks_matrix(blocks)
    for group in range(chunk_ref.shape[0] // (2 * size)):
        start, row = group * (2 * size), group * 16
        halves = [
            jnp.concatenate(
                [rows_ref[first : first + 8, LANES * b : LANES * (b + 1)] for b in range(blocks)], axis=0
            )
            for first in (row, row + 8)
        ]
        packed = jnp.dot(matrix, jnp.concatenate(halves, axis=1).astype(BF16), preferred_element_type=F32)
        chunk_ref[start : start + 2 * size, :] = jnp.concatenate(
            [packed[:, :LANES], packed[:, LANES:]], axis=0
        ).astype(BF16)
        if after is not None:
            after(group)


def choices(ids, values):
    lane = iota((ids.shape[0], LANES), 1).astype(ids.dtype)
    total = jnp.zeros((ids.shape[0], LANES), F32)
    for k in range(ids.shape[1]):
        total = total + jnp.where(ids[:, k : k + 1] == lane, values[k], 0.0)
    return total


def rank_of(ids):
    ids = ids.astype(jnp.int32)
    core, x, z, y = ids & 1, (ids >> 1) & 3, (ids >> 3) & 3, ids >> 5
    return ((core * 4 + y) * 4 + x) * 4 + z


def slot_of(chosen):
    rows = chosen.shape[0]
    before = jnp.where(iota((rows, rows), 1) < iota((rows, rows), 0), 1.0, 0.0).astype(BF16)
    return jnp.dot(before, chosen.astype(BF16), preferred_element_type=F32)


def interleave(first, second):
    experts = first.shape[1]
    expert, place = iota((experts, 2 * experts), 0), iota((experts, 2 * experts), 1)
    even = jnp.where(place == 2 * expert, 1.0, 0.0).astype(BF16)
    odd = jnp.where(place == 2 * expert + 1, 1.0, 0.0).astype(BF16)
    return jnp.dot(first.astype(BF16), even, preferred_element_type=F32) + jnp.dot(
        second.astype(BF16), odd, preferred_element_type=F32
    )


def dispatch_kernel(ids_hbm, hidden_hbm, chunk_ref, ids_ref, hidden_ref, rows_ref, sem):
    ids_copy = pltpu.make_async_copy(ids_hbm, ids_ref, sem.at[0])
    hidden_copy = pltpu.make_async_copy(hidden_hbm, hidden_ref, sem.at[1])
    ids_copy.start()
    hidden_copy.start()
    ids_copy.wait()
    count = ids_ref.shape[0]
    ids = jnp.transpose(ids_ref[...].astype(F32))
    width = hidden_ref.shape[1]
    counts = jnp.sum(choices(ids, [1.0] * count), axis=0, keepdims=True)
    chosen = choices(rank_of(ids), [1.0] * count)
    slot = slot_of(chosen)
    placer = interleave(jnp.where(slot == 0.0, chosen, 0.0), jnp.where(slot == 1.0, chosen, 0.0))
    placer = jnp.transpose(placer).astype(BF16)
    rows_ref[:, width:] = jnp.broadcast_to(counts, (rows_ref.shape[0], LANES))
    hidden_copy.wait()
    rows_ref[:, :width] = jnp.dot(placer, hidden_ref[...], preferred_element_type=F32)
    rows_to_chunks(rows_ref, chunk_ref, rows_ref.shape[1] // LANES)


def expert_kernel(
    chunk_ref,
    up_hbm,
    down_hbm,
    out_ref,
    load_ref,
    up_ref,
    down_ref,
    rows_ref,
    act_ref,
    made_ref,
    weight_sem,
):
    ups, downs = up_ref.shape[0], down_ref.shape[0]
    up_width, down_width = up_ref.shape[2], down_ref.shape[2]
    half = ups // 2
    width = up_ref.shape[1]

    copies = []
    for c in range(half):
        for part in (c, c + half):
            copies.append((up_hbm.at[0, :, pl.ds(part * up_width, up_width)], up_ref.at[part]))
    for c in range(downs):
        copies.append((down_hbm.at[0, :, pl.ds(c * down_width, down_width)], down_ref.at[c]))
    copies = [pltpu.make_async_copy(*pair, weight_sem.at[n]) for n, pair in enumerate(copies)]
    for copy in copies[:IN_FLIGHT]:
        copy.start()

    def arrive(n):
        copies[n].wait()
        if n + IN_FLIGHT < len(copies):
            copies[n + IN_FLIGHT].start()

    chunks_to_rows(chunk_ref, rows_ref, rows_ref.shape[1] // LANES)
    counts = jnp.sum(rows_ref[:, width:].astype(F32), axis=0, keepdims=True)
    load_ref[...] = counts * (0.5 / load_ref.shape[1])

    for c in range(half):
        arrive(2 * c)
        arrive(2 * c + 1)
        rows = rows_ref[:, :width]
        gate = jnp.dot(rows, up_ref[c], preferred_element_type=F32)
        up = jnp.dot(rows, up_ref[c + half], preferred_element_type=F32)
        act_ref[:, c * up_width : (c + 1) * up_width] = (gate / (1.0 + jnp.exp(-gate)) * up).astype(BF16)

    for c in range(downs):
        arrive(ups + c)
        made_ref[:, c * down_width : (c + 1) * down_width] = jnp.dot(
            act_ref[...], down_ref[c], preferred_element_type=F32
        )

    rows_to_chunks(made_ref, out_ref, made_ref.shape[1] // LANES)


def mixer_kernel(ids_ref, weights_ref, after_ref, mixer_ref):
    ids, weights = jnp.transpose(ids_ref[...].astype(F32)), jnp.transpose(weights_ref[...])
    count = ids.shape[1]
    ids = rank_of(ids)
    slot = slot_of(choices(ids, [1.0] * count))
    weight = choices(ids, [weights[:, k : k + 1] for k in range(count)])

    def parts(value):
        high = value.astype(BF16).astype(F32)
        return jnp.concatenate([high, value - high], axis=0)

    mixer = interleave(parts(jnp.where(slot == 0.0, weight, 0.0)), parts(jnp.where(slot == 1.0, weight, 0.0)))
    mixer_ref[...] = mixer.astype(BF16)


def combine_kernel(mixer_ref, chunk_hbm, out_ref, chunk_ref, rows_ref, sem):
    blocks = rows_ref.shape[1] // LANES
    pieces = sem.shape[0]
    span = chunk_ref.shape[0] // pieces
    enter = [
        pltpu.make_async_copy(
            chunk_hbm.at[pl.ds(n * span, span), :], chunk_ref.at[pl.ds(n * span, span), :], sem.at[n]
        )
        for n in range(pieces)
    ]
    for copy in enter:
        copy.start()
    groups = chunk_ref.shape[0] // (16 * blocks) // pieces

    def before(group):
        if group % groups == 0:
            enter[group // groups].wait()

    chunks_to_rows(chunk_ref, rows_ref, blocks, before)
    mixed = jnp.dot(mixer_ref[...], rows_ref[...], preferred_element_type=F32)
    rows = out_ref.shape[0]
    out_ref[...] = (mixed[:rows] + mixed[rows:]).astype(BF16)


def attend(query_latent, query_rope, latent_cache, rope_cache, cache_lengths):
    factor = (query_latent.shape[2] + query_rope.shape[1]) ** (-0.5)
    scores = jnp.einsum("rhc,rtc->rht", query_latent, latent_cache, preferred_element_type=F32)
    scores = scores + jnp.einsum("rph,rpt->rht", query_rope, rope_cache, preferred_element_type=F32)
    scores = scores * factor
    positions = jnp.arange(latent_cache.shape[1], dtype=jnp.int32)
    live_mask = positions[None, None, :] < cache_lengths[:, None, None]
    scores = jnp.where(live_mask, scores, -1e30)
    highest = jnp.max(scores, axis=-1, keepdims=True)
    powers = jnp.exp(scores - highest)
    attention_weights = (powers / jnp.sum(powers, axis=-1, keepdims=True)).astype(BF16)
    result = jnp.einsum("rht,rtc->rhc", attention_weights, latent_cache, preferred_element_type=F32)
    return result.astype(BF16)


def vmem(count):
    return [pl.BlockSpec(memory_space=pltpu.VMEM)] * count


def hbm(count):
    return [pl.BlockSpec(memory_space=pltpu.HBM)] * count


def exchange(chunks, experts):
    width = chunks.shape[1]
    shaped = chunks.reshape(experts, -1, 2, width)
    moved = lax.all_to_all(shaped, AXES, split_axis=0, concat_axis=0, tiled=True)
    return moved.reshape(chunks.shape)


def per_device(
    hidden,
    expert_ids,
    route_weights,
    w_gate_up,
    w_down,
    query_latent,
    query_rope,
    latent_cache,
    rope_cache,
    cache_lengths,
):
    model_width = hidden.shape[1]
    experts = lax.axis_size(AXES)
    slots = 2 * experts
    units = w_down.shape[1]
    blocks = model_width // LANES
    sent = blocks + 1

    outgoing = pl.pallas_call(
        dispatch_kernel,
        out_shape=jax.ShapeDtypeStruct((slots * sent, LANES), BF16),
        in_specs=hbm(2),
        out_specs=pl.BlockSpec(memory_space=pltpu.VMEM),
        scratch_shapes=[
            pltpu.VMEM(expert_ids.shape[::-1], jnp.int32),
            pltpu.VMEM(hidden.shape, BF16),
            pltpu.VMEM((slots, sent * LANES), F32),
            pltpu.SemaphoreType.DMA((2,)),
        ],
        compiler_params=pltpu.CompilerParams(vmem_limit_bytes=16 << 20),
        name="dispatch",
    )(expert_ids.T, hidden)
    received = exchange(outgoing, experts)

    up_width, down_width = 256, 1792
    ups, downs = 2 * units // up_width, model_width // down_width
    returned, load = pl.pallas_call(
        expert_kernel,
        out_shape=(
            jax.ShapeDtypeStruct((slots * blocks, LANES), BF16),
            jax.ShapeDtypeStruct((1, experts), F32),
        ),
        in_specs=vmem(1) + hbm(2),
        out_specs=tuple(vmem(2)),
        scratch_shapes=[
            pltpu.VMEM((ups, model_width, up_width), BF16),
            pltpu.VMEM((downs, units, down_width), BF16),
            pltpu.VMEM((slots, sent * LANES), BF16),
            pltpu.VMEM((slots, units), BF16),
            pltpu.VMEM((slots, model_width), F32),
            pltpu.SemaphoreType.DMA((ups + downs,)),
        ],
        compiler_params=pltpu.CompilerParams(vmem_limit_bytes=48 << 20),
        name="experts",
    )(received, w_gate_up, w_down)
    collected = exchange(returned, experts)

    mixer = pl.pallas_call(
        mixer_kernel,
        out_shape=jax.ShapeDtypeStruct((2 * hidden.shape[0], slots), BF16),
        in_specs=vmem(3),
        out_specs=pl.BlockSpec(memory_space=pltpu.VMEM),
        compiler_params=pltpu.CompilerParams(vmem_limit_bytes=4 << 20),
        name="mixer",
    )(expert_ids.T, route_weights.T, load)

    moe_out = pl.pallas_call(
        combine_kernel,
        out_shape=jax.ShapeDtypeStruct(hidden.shape, BF16),
        in_specs=vmem(1) + hbm(1),
        out_specs=pl.BlockSpec(memory_space=pltpu.VMEM),
        scratch_shapes=[
            pltpu.VMEM((slots * blocks, LANES), BF16),
            pltpu.VMEM((slots, model_width), BF16),
            pltpu.SemaphoreType.DMA((4,)),
        ],
        compiler_params=pltpu.CompilerParams(vmem_limit_bytes=16 << 20),
        name="combine",
    )(mixer, collected)
    attention_out = attend(query_latent, query_rope, latent_cache, rope_cache, cache_lengths)
    return (moe_out, load[0], attention_out)


def solution(mesh):
    split = ("y", "z", "x", "core")
    mesh = Mesh(mesh.devices.reshape(4, 4, 4, 2), split)
    return jax.shard_map(
        per_device,
        mesh=mesh,
        in_specs=(
            P(split, None),
            P(split, None),
            P(split, None),
            P(split, None, None),
            P(split, None, None),
            P(split, None, None),
            P(split, None, None),
            P(split, None, None),
            P(split, None, None),
            P(split),
        ),
        out_specs=(P(split, None), P(), P(split, None, None)),
        check_vma=False,
    )
```
